256 devices in a mesh: expert: 32 (over y, z), etp: 8 (over x, core).
Axes of the slice: x: 4, y: 4, z: 8, core: 2. Of those that a mesh axis runs over, the one named last changes fastest.
Arguments:
- tokens: bfloat16 [4096, 4096], P('expert', 'etp'), may hold values from -6 to 6
- expert_ids: int32 [4096, 8], P('expert'), may hold values from 0 to 63, all different within a row; in each aligned block of 128 rows (0 to 127, 128 to 255, ...) at most 24 rows name the same one
- gate_probs: float32 [4096, 8], P('expert'), may hold values from 0.1 to 0.5
- w_gate: bfloat16 [64, 1536, 4096], P('expert', 'etp'), may hold values from -0.09375 to 0.09375
- w_up: bfloat16 [64, 1536, 4096], P('expert', 'etp'), may hold values from -0.09375 to 0.09375
- w_down: bfloat16 [64, 1536, 4096], P('expert', None, 'etp'), may hold values from -0.15625 to 0.15625
Outputs:
- moe_out: bfloat16 [4096, 4096], P('expert', 'etp')
The draws below stay inside these ranges and needn't reach their ends.
Inputs may be any that keep to these rules, and one draw needn't show every extreme that they name: `expert_ids`: within each aligned block of 128 token rows (the rows of one index of expert), no expert is named by more than 24 rows, a bound that some block reaches; the 8 experts of a row differ.
All inputs are finite; a program needn't handle non-finite values.
Results may differ from the reference program's by a relative error of at most 0.0058.
Values may be sent and summed in bfloat16 or wider, within the bound.
No kernel may reach another device: no remote copies, remote signals or barrier semaphores. Data moves between devices by JAX's collectives and lax.ppermute only.
A program may use at most 128 MiB of HBM per device.

```python
import math
import jax
import jax.numpy as jnp
import numpy as np
from jax import lax

D = 4096
FF = 1536
TOPK = 8
TOK_DEV = 128
TOKENS = 4096
EXPERTS = 64
CAP = 24
N_EXPERT = 32


def level_of(rng, extent, pieces, least, top_value):
    gain = 1.0
    for axis_at, shards_of in pieces:
        steps = jax.random.uniform(jax.random.fold_in(jax.random.fold_in(rng, 6), axis_at), (shards_of,), jnp.float32, least / len(pieces), top_value / len(pieces))
        gain = gain * jnp.repeat(jnp.exp(steps), extent[axis_at] // shards_of).reshape((-1,) + (1,) * (len(extent) - 1 - axis_at))
    return gain


def assign_block(stream_key, own, number, rows, count, top, limit, slope):
    order = jax.random.permutation(stream_key, count)
    packed, usual = load_shares(count, rows * top, limit, slope, True), load_shares(count, rows * top, limit, slope, False)
    places = jnp.arange(count)

    def named(lengths, turn):
        used = int((lengths > 0).sum())
        fixed = max(1, used // 4)
        moved = fixed + (places - fixed + turn * (used - fixed)) % max(1, count - fixed)
        return jnp.zeros((count,), jnp.int32).at[order[jnp.where(places < fixed, places, moved)]].set(jnp.asarray(lengths, jnp.int32))

    lengths = jnp.where(number % 4 == 0, named(packed, number // 4), named(usual, number - number // 4 - 1))
    mixed = jax.random.permutation(jax.random.fold_in(own, 3), count)
    donor, receiver = mixed[0:count // 2 * 2:2], mixed[1:count // 2 * 2:2]
    margin = jnp.minimum(lengths[donor] - 1, limit - lengths[receiver]) // 2
    margin = jnp.where((donor == order[0]) | (receiver == order[0]) | (lengths[receiver] == 0), 0, jnp.maximum(margin, 0))
    moved = jax.random.randint(jax.random.fold_in(own, 4), (count // 2,), 0, 1 << 20) % (margin + 1)
    lengths = lengths.at[donor].add(-moved).at[receiver].add(moved)
    items = jnp.searchsorted(jnp.cumsum(lengths), jnp.arange(rows * top), side="right").astype(jnp.int32)
    grid = items.reshape(top, rows).T
    grid = grid[jax.random.permutation(jax.random.fold_in(own, 1), rows)]
    turn = jax.random.randint(jax.random.fold_in(own, 2), (rows, 1), 0, top)
    return jnp.take_along_axis(grid, (jnp.arange(top)[None, :] + turn) % top, axis=1)


def load_shares(number_of, total, reach, slope, full):
    loads = [(1 << 20) // math.isqrt(standing ** slope) + 1 for standing in range(1, number_of + 1)]
    largest = reach if full else min(reach, max(-(-total // number_of), total * loads[0] // sum(loads)))
    least = 1 if total - largest >= number_of - 1 else 0
    given, rest = [largest] + [least] * (number_of - 1), total - largest - least * (number_of - 1)
    while rest > 0:
        free = [i for i in range(1, number_of) if given[i] < largest] or [i for i in range(1, number_of) if given[i] < reach]
        mass, budget = sum([loads[i] for i in free]), rest
        for i in free:
            addition = min(reach - given[i], max(1, budget * loads[i] // mass), rest)
            given[i] = given[i] + addition
            rest = rest - addition
    return np.array(given)


def noise(own_key, dims, spread, limit, shards=(), kind=jnp.bfloat16):
    values = spread * jax.random.normal(own_key, dims, jnp.float32)
    if shards:
        values = values * level_of(own_key, dims, shards, -0.22, 0.18)
    return jnp.clip(values, -limit, limit).astype(kind)


def setup_inputs(seed: int = 0) -> dict:
    keys = jax.random.split(jax.random.key(seed), 7)
    tokens = noise(keys[0], (TOKENS, D), 1.0, 6.0, ((0, 32), (1, 8)))
    expert_ids_keys = jax.random.split(jax.random.fold_in(keys[1], 1), TOKENS // TOK_DEV)
    expert_ids_turns = jax.random.permutation(jax.random.fold_in(keys[1], 3), TOKENS // TOK_DEV)
    expert_ids = jax.vmap(lambda own, number: assign_block(jax.random.fold_in(keys[1], 2), own, number, TOK_DEV, EXPERTS, TOPK, CAP, 2))(expert_ids_keys, expert_ids_turns).reshape((TOKENS, TOPK))
    gate_probs = jnp.clip(0.1 + 0.4 * jax.random.uniform(keys[2], (TOKENS, TOPK), jnp.float32) ** level_of(keys[2], (TOKENS, TOPK), ((0, 32),), -0.2, 0.2), 0.1, 0.5)
    w_gate = noise(keys[3], (EXPERTS, FF, D), D ** -0.5, 0.09375, ((0, 32), (1, 8)))
    w_up = noise(keys[4], (EXPERTS, FF, D), D ** -0.5, 0.09375, ((0, 32), (1, 8)))
    w_down = noise(keys[5], (EXPERTS, FF, D), FF ** -0.5, 0.15625, ((0, 32), (2, 8)))
    return {"tokens": tokens, "expert_ids": expert_ids, "gate_probs": gate_probs, "w_gate": w_gate, "w_up": w_up, "w_down": w_down}


def reference(tokens, expert_ids, gate_probs, w_gate, w_up, w_down):
    blocks = N_EXPERT
    per_block = TOK_DEV * TOPK
    pairs = expert_ids.reshape(blocks, per_block)
    onehot = (pairs[:, :, None] == jnp.arange(EXPERTS, dtype=jnp.int32)[None, None, :]).astype(jnp.int32)
    position = jnp.sum(jnp.cumsum(onehot, axis=1) * onehot, axis=2) - 1
    block_index = jnp.arange(blocks, dtype=jnp.int32)[:, None]
    slot_index = ((pairs * blocks + block_index) * CAP + position).reshape(-1).astype(jnp.int32)
    total_slots = EXPERTS * blocks * CAP
    token_of = (jnp.arange(TOKENS * TOPK, dtype=jnp.int32) // TOPK).astype(jnp.int32)
    source_row = jnp.full((total_slots,), TOKENS, jnp.int32).at[slot_index].set(token_of)
    padded = jnp.concatenate([tokens, jnp.zeros((1, D), tokens.dtype)], axis=0)

    def one_expert(which):
        start = (which * blocks * CAP).astype(jnp.int32)
        rows_here = lax.dynamic_slice_in_dim(source_row, start, blocks * CAP)
        inputs = padded[rows_here]
        gate = lax.dot_general(inputs, w_gate[which], (((1,), (1,)), ((), ())), preferred_element_type=jnp.float32)
        upper = lax.dot_general(inputs, w_up[which], (((1,), (1,)), ((), ())), preferred_element_type=jnp.float32)
        hidden = (jax.nn.silu(gate) * upper).astype(jnp.bfloat16)
        return jnp.dot(hidden, w_down[which], preferred_element_type=jnp.float32).astype(jnp.bfloat16)

    results = lax.map(one_expert, jnp.arange(EXPERTS, dtype=jnp.int32))
    results = results.reshape(total_slots, D)
    picked = results[slot_index].astype(jnp.float32).reshape(TOKENS, TOPK, D)
    mixed = jnp.sum(picked * gate_probs[:, :, None], axis=1)
    return mixed.astype(jnp.bfloat16)
```

```python
import jax
import jax.numpy as jnp
from jax import lax
from jax.sharding import PartitionSpec as P

BF16 = jnp.bfloat16
F32 = jnp.float32


def dot(a, b, dims):
    return lax.dot_general(a, b, ((dims[0], dims[1]), ((), ())), preferred_element_type=F32)


def routing(expert_ids, gate_probs, expert_count, capacity):
    tok_rows = expert_ids.shape[0]
    experts = jnp.arange(expert_count, dtype=jnp.int32)[:, None, None]
    hit = expert_ids.T[None] == experts
    member = jnp.any(hit, axis=1)
    gate = jnp.sum(jnp.where(hit, gate_probs.T[None], 0.0), axis=1)
    earlier = jnp.arange(tok_rows)[:, None] < jnp.arange(tok_rows)[None, :]
    position = dot(member.astype(BF16), earlier.astype(BF16), ((1,), (0,)))
    position = jnp.where(member, position, -1.0)
    chosen = position[:, None, :] == jnp.arange(capacity, dtype=F32)[None, :, None]
    high = lax.reduce_precision(gate, 8, 7)
    low = gate - high
    pick = chosen.astype(BF16)
    scale = jnp.concatenate([high, low], axis=1).astype(BF16)
    both = jnp.concatenate([chosen, chosen], axis=2)
    mix = jnp.where(both, scale[:, None, :], jnp.zeros((), BF16))
    return pick, mix


def on_device(tokens, expert_ids, gate_probs, w_gate, w_up, w_down):
    tok_rows, width = tokens.shape
    top_count = expert_ids.shape[1]
    owners = lax.axis_size("expert")
    local_experts = w_gate.shape[0]
    expert_count = owners * local_experts
    capacity = 3 * tok_rows * top_count // (2 * expert_count)
    pick, mix = routing(expert_ids, gate_probs, expert_count, capacity)
    pick = pick.reshape(owners, local_experts, capacity, tok_rows)
    mix = mix.reshape(owners, local_experts, capacity, 2 * tok_rows)
    total = jnp.zeros((tok_rows, width), F32)
    slots = owners * capacity
    for j in range(local_experts):
        sel = pick[:, j].reshape(slots, tok_rows)
        outgoing = dot(sel, tokens, ((1,), (0,))).astype(BF16).reshape(owners, capacity, width)
        arrived = lax.all_to_all(outgoing, "expert", 0, 0, tiled=True).reshape(slots, width)
        rows = lax.all_gather(arrived, "etp", axis=1, tiled=True)
        gate = dot(w_gate[j], rows, ((1,), (1,)))
        upper = dot(w_up[j], rows, ((1,), (1,)))
        hidden = (jax.nn.silu(gate) * upper).astype(BF16)
        hidden_all = lax.all_gather(hidden, "etp", axis=0, tiled=True)
        result = dot(hidden_all, w_down[j], ((0,), (0,))).astype(BF16)
        returned = lax.all_to_all(
            result.reshape(owners, capacity, width), "expert", 0, 0, tiled=True
        ).reshape(slots, width)
        parts = dot(mix[:, j].reshape(slots, 2 * tok_rows), returned, ((0,), (0,)))
        total = total + parts[:tok_rows] + parts[tok_rows:]
    return total.astype(BF16)


def solution(mesh):
    return jax.shard_map(
        on_device,
        mesh=mesh,
        in_specs=(
            P("expert", "etp"),
            P("expert", None),
            P("expert", None),
            P("expert", "etp", None),
            P("expert", "etp", None),
            P("expert", None, "etp"),
        ),
        out_specs=P("expert", "etp"),
        check_vma=False,
    )
```

```python
import functools

import jax
import jax.numpy as jnp
from jax import lax
from jax.experimental import pallas as pl
from jax.experimental.pallas import tpu as pltpu
from jax.sharding import PartitionSpec as P

BF16 = jnp.bfloat16
F32 = jnp.float32
CORES = 2
TILE = 256


def dot(a, b, dims):
    return lax.dot_general(a, b, (dims, ((), ())), preferred_element_type=F32)


def routing(expert_ids, gate_probs, expert_count, capacity):
    tok_rows = expert_ids.shape[0]
    experts = jnp.arange(expert_count, dtype=jnp.int32)[:, None, None]
    hit = expert_ids.T[None] == experts
    member = jnp.any(hit, axis=1)
    gate = jnp.sum(jnp.where(hit, gate_probs.T[None], 0.0), axis=1)
    earlier = jnp.arange(tok_rows)[:, None] < jnp.arange(tok_rows)[None, :]
    position = dot(member.astype(BF16), earlier.astype(BF16), ((1,), (0,)))
    position = jnp.where(member, position, -1.0)
    chosen = position[:, None, :] == jnp.arange(capacity, dtype=F32)[None, :, None]
    high = lax.reduce_precision(gate, 8, 7)
    low = gate - high
    pick = chosen.astype(BF16)
    scale = jnp.concatenate([high, low], axis=1).astype(BF16)
    both = jnp.concatenate([chosen, chosen], axis=2)
    mix = jnp.where(both, scale[:, None, :], jnp.zeros((), BF16))
    return pick, mix


def hop(value, dx, flip):
    size = lax.axis_size("etp")
    chips = size // CORES
    pairs = []
    for x in range(chips):
        for c in range(CORES):
            pairs.append((x * CORES + c, ((x + dx) % chips) * CORES + (c ^ flip)))
    return lax.ppermute(value, "etp", pairs)


def gather_blocks(own):
    chips = lax.axis_size("etp") // CORES
    direct = [own] + [hop(own, dx, 0) for dx in range(1, chips)]
    return direct + [hop(b, 0, 1) for b in direct]


def block_places():
    size = lax.axis_size("etp")
    chips = size // CORES
    me = lax.axis_index("etp")
    x, c = me // CORES, me % CORES
    back = [lax.rem(x + chips - dx, chips) for dx in range(chips)]
    return [b * CORES + c for b in back] + [b * CORES + (1 - c) for b in back]


def gate_up_kernel(j, count, *refs):
    blocks = refs[:count]
    wg, wu, out, rows, weights, sems, wsems = refs[count:]
    ff = wg.shape[1]
    width = blocks[0].shape[1]
    tiles = blocks[0].shape[0] // TILE
    wcopies = [
        pltpu.make_async_copy(wg.at[j], weights.at[pl.ds(0, ff)], wsems.at[0]),
        pltpu.make_async_copy(wu.at[j], weights.at[pl.ds(ff, ff)], wsems.at[1]),
    ]
    for w in wcopies:
        w.start()
    places = block_places()
    copies = []
    for i in range(tiles):
        for b in range(count):
            lane = pl.multiple_of(places[b] * width, width)
            copies.append(
                pltpu.make_async_copy(
                    blocks[b].at[pl.ds(i * TILE, TILE)],
                    rows.at[pl.ds(i * TILE, TILE), pl.ds(lane, width)],
                    sems.at[i, b],
                )
            )
    for cp in copies:
        cp.start()
    for w in wcopies:
        w.wait()
    for i in range(tiles):
        for b in range(count):
            copies[i * count + b].wait()
        both = dot(weights[...], rows[pl.ds(i * TILE, TILE), :], ((1,), (1,)))
        gate, upper = both[:ff], both[ff:]
        out[:, pl.ds(i * TILE, TILE)] = (gate / (1.0 + jnp.exp(-gate)) * upper).astype(BF16)


def gate_up(blocks, w_gate, w_up, j):
    count = len(blocks)
    slots, width = blocks[0].shape
    ff = w_gate.shape[1]
    depth = w_gate.shape[2]
    tiles = slots // TILE
    return pl.pallas_call(
        functools.partial(gate_up_kernel, j, count),
        out_shape=jax.ShapeDtypeStruct((ff, slots), BF16),
        in_specs=[pl.BlockSpec(memory_space=pl.ANY)] * (count + 2),
        out_specs=pl.BlockSpec(memory_space=pltpu.VMEM),
        scratch_shapes=[
            pltpu.VMEM((slots, depth), BF16),
            pltpu.VMEM((2 * ff, depth), BF16),
            pltpu.SemaphoreType.DMA((tiles, count)),
            pltpu.SemaphoreType.DMA((2,)),
        ],
        compiler_params=pltpu.CompilerParams(vmem_limit_bytes=32 * 1024 * 1024),
        cost_estimate=pl.CostEstimate(
            flops=4 * slots * depth * ff,
            bytes_accessed=2 * depth * (slots + 2 * ff),
            transcendentals=slots * ff,
        ),
        name="gate_up",
    )(*blocks, w_gate, w_up)


def down_kernel(j, count, *refs):
    blocks = refs[:count]
    wd, out, hidden, weights, sems, wsem = refs[count:]
    ff = blocks[0].shape[0]
    slots = blocks[0].shape[1]
    wcopy = pltpu.make_async_copy(wd.at[j], weights, wsem)
    wcopy.start()
    places = block_places()
    copies = []
    for b in range(count):
        at = pl.multiple_of(places[b] * ff, ff)
        copies.append(pltpu.make_async_copy(blocks[b], hidden.at[pl.ds(at, ff)], sems.at[b]))
    for cp in copies:
        cp.start()
    wcopy.wait()
    for cp in copies:
        cp.wait()
    for i in range(slots // TILE):
        part = dot(hidden[:, pl.ds(i * TILE, TILE)], weights[...], ((0,), (0,)))
        out[pl.ds(i * TILE, TILE), :] = part.astype(BF16)


def down(blocks, w_down, j):
    count = len(blocks)
    ff, slots = blocks[0].shape
    depth, width = w_down.shape[1:]
    return pl.pallas_call(
        functools.partial(down_kernel, j, count),
        out_shape=jax.ShapeDtypeStruct((slots, width), BF16),
        in_specs=[pl.BlockSpec(memory_space=pl.ANY)] * (count + 1),
        out_specs=pl.BlockSpec(memory_space=pltpu.VMEM),
        scratch_shapes=[
            pltpu.VMEM((depth, slots), BF16),
            pltpu.VMEM((depth, width), BF16),
            pltpu.SemaphoreType.DMA((count,)),
            pltpu.SemaphoreType.DMA,
        ],
        compiler_params=pltpu.CompilerParams(vmem_limit_bytes=24 * 1024 * 1024),
        cost_estimate=pl.CostEstimate(
            flops=2 * slots * depth * width,
            bytes_accessed=2 * (depth * slots + depth * width + slots * width),
            transcendentals=0,
        ),
        name="down",
    )(*blocks, w_down)


def on_device(tokens, expert_ids, gate_probs, w_gate, w_up, w_down):
    tok_rows, width = tokens.shape
    top_count = expert_ids.shape[1]
    owners = lax.axis_size("expert")
    local_experts = w_gate.shape[0]
    expert_count = owners * local_experts
    capacity = 3 * tok_rows * top_count // (2 * expert_count)
    pick, mix = routing(expert_ids, gate_probs, expert_count, capacity)
    pick = pick.reshape(owners, local_experts, capacity, tok_rows)
    mix = mix.reshape(owners, local_experts, capacity, 2 * tok_rows)
    total = jnp.zeros((tok_rows, width), F32)
    slots = owners * capacity
    for j in range(local_experts):
        sel = pick[:, j].reshape(slots, tok_rows)
        outgoing = dot(sel, tokens, ((1,), (0,))).astype(BF16).reshape(owners, capacity, width)
        arrived = lax.all_to_all(outgoing, "expert", 0, 0, tiled=True).reshape(slots, width)
        hidden = gate_up(gather_blocks(arrived), w_gate, w_up, j)
        result = down(gather_blocks(hidden), w_down, j)
        returned = lax.all_to_all(
            result.reshape(owners, capacity, width), "expert", 0, 0, tiled=True
        ).reshape(slots, width)
        parts = dot(mix[:, j].reshape(slots, 2 * tok_rows), returned, ((0,), (0,)))
        total = total + parts[:tok_rows] + parts[tok_rows:]
    return total.astype(BF16)


def solution(mesh):
    return jax.shard_map(
        on_device,
        mesh=mesh,
        in_specs=(
            P("expert", "etp"),
            P("expert", None),
            P("expert", None),
            P("expert", "etp", None),
            P("expert", "etp", None),
            P("expert", None, "etp"),
        ),
        out_specs=P("expert", "etp"),
        check_vma=False,
    )
```

```python
import functools

import jax
import jax.numpy as jnp
from jax import lax
from jax.experimental import pallas as pl
from jax.experimental.pallas import tpu as pltpu
from jax.sharding import PartitionSpec as P


BF16 = jnp.bfloat16
F32 = jnp.float32
CORES = 2
TILE = 256
PARTS = 2
VMEM = 16 * 1024 * 1024


def dot(a, b, dims):
    return lax.dot_general(a, b, (dims, ((), ())), preferred_element_type=F32)


def routing(expert_ids, gate_probs, expert_count, owners):
    tok_rows = expert_ids.shape[0]
    experts = jnp.arange(expert_count, dtype=jnp.int32)[:, None, None]
    hit = expert_ids.T[None] == experts
    member = jnp.any(hit, axis=1)
    gate = jnp.sum(jnp.where(hit, gate_probs.T[None], 0.0), axis=1)
    earlier = jnp.arange(tok_rows)[:, None] < jnp.arange(tok_rows)[None, :]
    position = dot(member.astype(BF16), earlier.astype(BF16), ((1,), (0,)))
    position = jnp.where(member, position, -1.0).reshape(owners, -1, 1, tok_rows)
    high = lax.reduce_precision(gate, 8, 7)
    low = (gate - high).astype(BF16).reshape(position.shape)
    return position, high.astype(BF16).reshape(position.shape), low


def matrices(position, high, low, runs):
    pick, mix = [], []
    for j, first, length in runs:
        slot = jnp.arange(first, first + length, dtype=jnp.int32).astype(F32)[None, :, None]
        chosen = position[:, j] == slot
        zero = jnp.zeros((), BF16)
        pick.append(chosen.astype(BF16))
        mix.append(jnp.concatenate([jnp.where(chosen, high[:, j], zero), jnp.where(chosen, low[:, j], zero)], axis=2))
    return jnp.concatenate(pick, axis=1), jnp.concatenate(mix, axis=1)


def hop(value, dx, flip):
    size = lax.axis_size("etp")
    chips = size // CORES
    pairs = []
    for x in range(chips):
        for c in range(CORES):
            pairs.append((x * CORES + c, ((x + dx) % chips) * CORES + (c ^ flip)))
    return lax.ppermute(value, "etp", pairs)


def in_hbm(value):
    return pltpu.with_memory_space_constraint(value, pltpu.HBM)


def swap(value):
    return hop(value, 0, 1)


def places(steps):
    chips = lax.axis_size("etp") // CORES
    me = lax.axis_index("etp")
    x, c = me // CORES, me % CORES
    back = [lax.rem(x + chips - dx, chips) * CORES for dx in steps]
    return [b + c for b in back] + [b + 1 - c for b in back]


def pick_expert(values, axis, group):
    if len(values) == 1:
        return values[0]
    slot = lax.broadcasted_iota(jnp.int32, values[0].shape, axis)
    turn = lax.rem(slot // group, len(values))
    out = values[0]
    for n in range(1, len(values)):
        out = jnp.where(turn == n, values[n], out)
    return out


def product_kernel(experts, group, steps, split, last, *refs):
    count = CORES * len(steps)
    pieces = refs[: count * split]
    rest = refs[count * split :]
    if last:
        wg, wu, prior, out, rows, weights, sems, wsems = rest
    else:
        wg, wu, out, rows, weights, sems, wsems = rest
    ff = wg.shape[1]
    height, width = pieces[0].shape
    copies = []
    for b, place in enumerate(places(steps)):
        lane = pl.multiple_of(place * width, width)
        for n, j in enumerate(experts):
            for half, w in enumerate((wg, wu)):
                copies.append(
                    pltpu.make_async_copy(
                        w.at[j, :, pl.ds(lane, width)],
                        weights.at[n, pl.ds(half * ff, ff), pl.ds(b * width, width)],
                        wsems.at[n, b, half],
                    )
                )

    tiles = height * split // TILE
    per = max(1, tiles // split) if split == 1 else 1
    step = height // per

    def pulls(i):
        out = []
        for b in range(count):
            for p in range(split):
                out.append(
                    pltpu.make_async_copy(
                        pieces[b * split + p].at[pl.ds(pl.multiple_of(i * step, step), step)],
                        rows.at[pl.ds(pl.multiple_of(p * height + i * step, step), step), pl.ds(b * width, width)],
                        sems.at[i, b, p],
                    )
                )
        return out

    for cp in copies:
        cp.start()
    for i in range(per):
        for cp in pulls(i):
            cp.start()
    for cp in copies:
        cp.wait()
    if per == 1:
        for cp in pulls(0):
            cp.wait()

    @pl.loop(0, tiles)
    def _(i):
        if per > 1:
            for cp in pulls(i):
                cp.wait()
        at = pl.ds(pl.multiple_of(i * TILE, TILE), TILE)
        both = [dot(weights[n], rows[at, :], ((1,), (1,))) for n in range(len(experts))]
        both = pick_expert(both, 1, group)
        if last:
            both = both + prior[:, at]
            gate, upper = both[:ff], both[ff:]
            out[:, at] = (gate / (1.0 + jnp.exp(-gate)) * upper).astype(BF16)
        else:
            out[:, at] = both


def product(pieces, steps, split, w_gate, w_up, experts, group, prior=None):
    count = CORES * len(steps)
    height, width = pieces[0].shape
    slots = height * split
    ff = w_gate.shape[1]
    last = prior is not None
    hbm = pl.BlockSpec(memory_space=pl.ANY)
    vmem = pl.BlockSpec(memory_space=pltpu.VMEM)
    shape = jax.ShapeDtypeStruct((ff, slots), BF16) if last else jax.ShapeDtypeStruct((2 * ff, slots), F32)
    return pl.pallas_call(
        functools.partial(product_kernel, experts, group, steps, split, last),
        out_shape=shape,
        in_specs=[hbm] * (len(pieces) + 2) + ([vmem] if last else []),
        out_specs=vmem,
        scratch_shapes=[
            pltpu.VMEM((slots, count * width), BF16),
            pltpu.VMEM((len(experts), 2 * ff, count * width), BF16),
            pltpu.SemaphoreType.DMA((slots // TILE, count, split)),
            pltpu.SemaphoreType.DMA((len(experts), count, 2)),
        ],
        compiler_params=pltpu.CompilerParams(vmem_limit_bytes=VMEM),
        cost_estimate=pl.CostEstimate(
            flops=4 * slots * count * width * ff,
            bytes_accessed=2 * count * width * (slots + 2 * ff) + 4 * 2 * ff * slots,
            transcendentals=slots * ff if last else 0,
        ),
        name="gate_up_last" if last else "gate_up_first",
    )(*pieces, in_hbm(w_gate), in_hbm(w_up), *([prior] if last else []))


def gate_up(own, w_gate, w_up, experts, group, far=None):
    half = own.shape[0] // 2
    ahead, behind, partner = hop(own, 1, 0), hop(own, -1, 0), swap(own)
    if far is None:
        far = [hop(ahead[:half], 1, 0), hop(behind[half:], -1, 0)]
        early, early_steps, late_steps, split = True, (0, 1, -1), (2,), 2
    else:
        far, early, early_steps, late_steps, split = [far], False, (0,), (1, -1, 2), 1
    swapped = [swap(ahead), swap(behind)]
    far_swapped = [swap(b) for b in far]
    if early:
        first, last = [own, ahead, behind, partner, *swapped], far + far_swapped
    else:
        first, last = [own, partner], [ahead, behind, *far, *swapped, *far_swapped]
    first = product(first, early_steps, 1, w_gate, w_up, experts, group)
    return product(last, late_steps, split, w_gate, w_up, experts, group, first)


def down_kernel(experts, group, count, *refs):
    blocks = refs[:count]
    wd, out, hidden, weights, result, sems, wsems, osems = refs[count:]
    ff, slots = blocks[0].shape
    copies = [pltpu.make_async_copy(wd.at[j], weights.at[n], wsems.at[n]) for n, j in enumerate(experts)]
    for b, place in enumerate(places(range(count // CORES))):
        at = pl.multiple_of(place * ff, ff)
        copies.append(pltpu.make_async_copy(blocks[b], hidden.at[pl.ds(at, ff)], sems.at[b]))
    for cp in copies:
        cp.start()
    for cp in copies:
        cp.wait()

    outs = []
    for i in range(slots // TILE):
        at = pl.ds(i * TILE, TILE)
        part = [dot(hidden[:, at], weights[n], ((0,), (0,))) for n in range(len(experts))]
        result[at, :] = pick_expert(part, 0, group).astype(BF16)
        outs.append(pltpu.make_async_copy(result.at[at], out.at[at], osems.at[i]))
        outs[-1].start()
    for cp in outs:
        cp.wait()


def down(hidden, w_down, experts, group):
    chips = lax.axis_size("etp") // CORES
    blocks = [hidden] + [hop(hidden, dx, 0) for dx in range(1, chips)]
    partner = swap(hidden)
    blocks = blocks + [partner] + [swap(b) for b in blocks[1:]]
    count = len(blocks)
    _, slots = hidden.shape
    depth, width = w_down.shape[1:]
    hbm = pl.BlockSpec(memory_space=pl.ANY)
    return pl.pallas_call(
        functools.partial(down_kernel, experts, group, count),
        out_shape=jax.ShapeDtypeStruct((slots, width), BF16),
        in_specs=[hbm] * (count + 1),
        out_specs=hbm,
        scratch_shapes=[
            pltpu.VMEM((depth, slots), BF16),
            pltpu.VMEM((len(experts), depth, width), BF16),
            pltpu.VMEM((slots, width), BF16),
            pltpu.SemaphoreType.DMA((count,)),
            pltpu.SemaphoreType.DMA((len(experts),)),
            pltpu.SemaphoreType.DMA((slots // TILE,)),
        ],
        compiler_params=pltpu.CompilerParams(vmem_limit_bytes=VMEM),
        cost_estimate=pl.CostEstimate(
            flops=2 * slots * depth * width,
            bytes_accessed=2 * (depth * slots + depth * width + slots * width),
            transcendentals=0,
        ),
        name="down",
    )(*blocks, in_hbm(w_down))


def chunks_of(local_experts, capacity):
    size = local_experts * capacity // PARTS
    chunks = []
    for q in range(PARTS):
        runs, at = [], q * size
        while at < (q + 1) * size:
            j, c = at // capacity, at % capacity
            length = min((q + 1) * size - at, capacity - c)
            runs.append((j, c, length))
            at += length
        chunks.append(runs)
    return chunks


def layer(tokens, expert_ids, gate_probs, w_gate, w_up, w_down):
    tok_rows, width = tokens.shape
    top_count = expert_ids.shape[1]
    owners = lax.axis_size("expert")
    local_experts = w_gate.shape[0]
    expert_count = owners * local_experts
    capacity = 3 * tok_rows * top_count // (2 * expert_count)
    route = routing(expert_ids, gate_probs, expert_count, owners)
    size = local_experts * capacity // PARTS
    slots = owners * size
    total = jnp.zeros((tok_rows, width), F32)
    far_tokens = hop(tokens, lax.axis_size("etp") // CORES // 2, 0)

    def send(pick, rows):
        outgoing = dot(pick.reshape(slots, tok_rows), rows, ((1,), (0,))).astype(BF16)
        return lax.all_to_all(outgoing.reshape(owners, size, width), "expert", 0, 0, tiled=True)

    for q, runs in enumerate(chunks_of(local_experts, capacity)):
        experts = tuple(j for j, _, _ in runs)
        group = runs[0][2]
        pick, mix = matrices(*route, runs)
        arrived = send(pick, tokens).reshape(slots, width)
        far = send(pick, far_tokens).reshape(slots, width) if q else None
        hidden = gate_up(arrived, w_gate, w_up, experts, group, far)
        result = down(hidden, w_down, experts, group).reshape(owners, size, width)
        returned = lax.all_to_all(result, "expert", 0, 0, tiled=True).reshape(slots, width)
        parts = dot(mix.reshape(slots, 2 * tok_rows), returned, ((0,), (0,)))
        total = total + parts[:tok_rows] + parts[tok_rows:]
    return total.astype(BF16)


def solution(mesh):
    return jax.shard_map(
        layer,
        mesh=mesh,
        in_specs=(
            P("expert", "etp"),
            P("expert", None),
            P("expert", None),
            P("expert", "etp", None),
            P("expert", "etp", None),
            P("expert", None, "etp"),
        ),
        out_specs=P("expert", "etp"),
        check_vma=False,
    )
```

```python
import functools

import jax
import jax.numpy as jnp
from jax import lax
from jax.experimental import pallas as pl
from jax.experimental.pallas import tpu as pltpu
from jax.sharding import PartitionSpec as P


BF16 = jnp.bfloat16
F32 = jnp.float32
CORES = 2
TILE = 256
PARTS = 2
VMEM = 16 * 1024 * 1024


def dot(a, b, dims):
    return lax.dot_general(a, b, (dims, ((), ())), preferred_element_type=F32)


def routing(expert_ids, gate_probs, expert_count, owners):
    tok_rows = expert_ids.shape[0]
    experts = jnp.arange(expert_count, dtype=jnp.int32)[:, None, None]
    hit = expert_ids.T[None] == experts
    member = jnp.any(hit, axis=1)
    gate = jnp.sum(jnp.where(hit, gate_probs.T[None], 0.0), axis=1)
    earlier = jnp.arange(tok_rows)[:, None] < jnp.arange(tok_rows)[None, :]
    position = dot(member.astype(BF16), earlier.astype(BF16), ((1,), (0,)))
    position = jnp.where(member, position, -1.0).reshape(owners, -1, 1, tok_rows)
    high = lax.reduce_precision(gate, 8, 7)
    low = (gate - high).astype(BF16).reshape(position.shape)
    return position, high.astype(BF16).reshape(position.shape), low


def matrices(position, high, low, runs):
    pick, mix = [], []
    for j, first, length in runs:
        slot = jnp.arange(first, first + length, dtype=jnp.int32).astype(F32)[None, :, None]
        chosen = position[:, j] == slot
        zero = jnp.zeros((), BF16)
        pick.append(chosen.astype(BF16))
        mix.append(jnp.concatenate([jnp.where(chosen, high[:, j], zero), jnp.where(chosen, low[:, j], zero)], axis=2))
    return jnp.concatenate(pick, axis=1), jnp.concatenate(mix, axis=1)


def hop(value, dx, flip):
    size = lax.axis_size("etp")
    chips = size // CORES
    pairs = []
    for x in range(chips):
        for c in range(CORES):
            pairs.append((x * CORES + c, ((x + dx) % chips) * CORES + (c ^ flip)))
    return lax.ppermute(value, "etp", pairs)


def in_hbm(value):
    return pltpu.with_memory_space_constraint(value, pltpu.HBM)


def swap(value):
    return hop(value, 0, 1)


def places(steps):
    chips = lax.axis_size("etp") // CORES
    me = lax.axis_index("etp")
    x, c = me // CORES, me % CORES
    back = [lax.rem(x + chips - dx, chips) * CORES for dx in steps]
    return [b + c for b in back] + [b + 1 - c for b in back]


def pick_expert(values, axis, group):
    if len(values) == 1:
        return values[0]
    slot = lax.broadcasted_iota(jnp.int32, values[0].shape, axis)
    turn = lax.rem(slot // group, len(values))
    out = values[0]
    for n in range(1, len(values)):
        out = jnp.where(turn == n, values[n], out)
    return out


def product_kernel(experts, group, steps, wide, split, last, *refs):
    count = CORES * len(steps)
    pieces = refs[: count * split // wide]
    rest = refs[count * split // wide :]
    if last:
        wg, wu, prior, out, rows, weights, sems, wsems = rest
    else:
        wg, wu, out, rows, weights, sems, wsems = rest
    ff = wg.shape[1]
    height, width = pieces[0].shape[0], pieces[0].shape[1] // wide
    copies = []
    for b, place in enumerate(places(steps)):
        lane = pl.multiple_of(place * width, width)
        for n, j in enumerate(experts):
            for half, w in enumerate((wg, wu)):
                copies.append(
                    pltpu.make_async_copy(
                        w.at[j, :, pl.ds(lane, width)],
                        weights.at[n, pl.ds(half * ff, ff), pl.ds(b * width, width)],
                        wsems.at[n, b, half],
                    )
                )

    tiles = height * split // TILE
    per = max(1, tiles // split) if split == 1 else 1
    step = height // per

    def pulls(i):
        out = []
        for b in range(count):
            for p in range(split):
                out.append(
                    pltpu.make_async_copy(
                        pieces[b // wide * split + p].at[
                            pl.ds(pl.multiple_of(i * step, step), step), pl.ds(b % wide * width, width)
                        ],
                        rows.at[pl.ds(pl.multiple_of(p * height + i * step, step), step), pl.ds(b * width, width)],
                        sems.at[i, b, p],
                    )
                )
        return out

    for cp in copies:
        cp.start()
    for i in range(per):
        for cp in pulls(i):
            cp.start()
    for cp in copies:
        cp.wait()
    if per == 1:
        for cp in pulls(0):
            cp.wait()

    @pl.loop(0, tiles)
    def _(i):
        if per > 1:
            for cp in pulls(i):
                cp.wait()
        at = pl.ds(pl.multiple_of(i * TILE, TILE), TILE)
        both = [dot(weights[n], rows[at, :], ((1,), (1,))) for n in range(len(experts))]
        both = pick_expert(both, 1, group)
        if last:
            both = both + prior[:, at]
            gate, upper = both[:ff], both[ff:]
            out[:, at] = (gate / (1.0 + jnp.exp(-gate)) * upper).astype(BF16)
        else:
            out[:, at] = both


def product(pieces, wide, steps, split, w_gate, w_up, experts, group, prior=None):
    count = CORES * len(steps)
    height, width = pieces[0].shape[0], pieces[0].shape[1] // wide
    slots = height * split
    ff = w_gate.shape[1]
    last = prior is not None
    hbm = pl.BlockSpec(memory_space=pl.ANY)
    vmem = pl.BlockSpec(memory_space=pltpu.VMEM)
    shape = jax.ShapeDtypeStruct((ff, slots), BF16) if last else jax.ShapeDtypeStruct((2 * ff, slots), F32)
    return pl.pallas_call(
        functools.partial(product_kernel, experts, group, steps, wide, split, last),
        out_shape=shape,
        in_specs=[hbm] * (len(pieces) + 2) + ([vmem] if last else []),
        out_specs=vmem,
        scratch_shapes=[
            pltpu.VMEM((slots, count * width), BF16),
            pltpu.VMEM((len(experts), 2 * ff, count * width), BF16),
            pltpu.SemaphoreType.DMA((slots // TILE, count, split)),
            pltpu.SemaphoreType.DMA((len(experts), count, 2)),
        ],
        compiler_params=pltpu.CompilerParams(vmem_limit_bytes=VMEM),
        cost_estimate=pl.CostEstimate(
            flops=4 * slots * count * width * ff,
            bytes_accessed=2 * count * width * (slots + 2 * ff) + 4 * 2 * ff * slots,
            transcendentals=slots * ff if last else 0,
        ),
        name="gate_up_last" if last else "gate_up_first",
    )(*pieces, in_hbm(w_gate), in_hbm(w_up), *([prior] if last else []))


def gate_up(arrived, width, w_gate, w_up, experts, group):
    wide = arrived.shape[1] // width
    own = arrived[:, :width]
    half = own.shape[0] // 2
    ahead, behind = hop(own, 1, 0), hop(own, -1, 0)
    partner = swap(arrived)
    swapped = [swap(ahead), swap(behind)]
    if wide == 1:
        far = [hop(ahead[:half], 1, 0), hop(behind[half:], -1, 0)]
        late = far + [swap(b) for b in far]
        early, early_steps, late_steps, split = [own, ahead, behind, partner, *swapped], (0, 1, -1), (2,), 2
    else:
        early, late = [arrived, partner], [ahead, behind, *swapped]
        early_steps, late_steps, split = (0, 2), (1, -1), 1
    first = product(early, wide, early_steps, 1, w_gate, w_up, experts, group)
    return product(late, 1, late_steps, split, w_gate, w_up, experts, group, first)


def down_kernel(experts, group, count, *refs):
    blocks = refs[:count]
    wd, out, hidden, weights, result, sems, wsems, osems = refs[count:]
    ff, slots = blocks[0].shape
    copies = [pltpu.make_async_copy(wd.at[j], weights.at[n], wsems.at[n]) for n, j in enumerate(experts)]
    for b, place in enumerate(places(range(count // CORES))):
        at = pl.multiple_of(place * ff, ff)
        copies.append(pltpu.make_async_copy(blocks[b], hidden.at[pl.ds(at, ff)], sems.at[b]))
    for cp in copies:
        cp.start()
    for cp in copies:
        cp.wait()

    outs = []
    for i in range(slots // TILE):
        at = pl.ds(i * TILE, TILE)
        part = [dot(hidden[:, at], weights[n], ((0,), (0,))) for n in range(len(experts))]
        result[at, :] = pick_expert(part, 0, group).astype(BF16)
        outs.append(pltpu.make_async_copy(result.at[at], out.at[at], osems.at[i]))
        outs[-1].start()
    for cp in outs:
        cp.wait()


def down(hidden, w_down, experts, group):
    one, back = hop(hidden, 1, 0), hop(hidden, -1, 0)
    blocks = [hidden, one, hop(hidden, 2, 0), back]
    partner = swap(hidden)
    blocks = blocks + [partner] + [swap(b) for b in blocks[1:]]
    count = len(blocks)
    _, slots = hidden.shape
    depth, width = w_down.shape[1:]
    hbm = pl.BlockSpec(memory_space=pl.ANY)
    return pl.pallas_call(
        functools.partial(down_kernel, experts, group, count),
        out_shape=jax.ShapeDtypeStruct((slots, width), BF16),
        in_specs=[hbm] * (count + 1),
        out_specs=hbm,
        scratch_shapes=[
            pltpu.VMEM((depth, slots), BF16),
            pltpu.VMEM((len(experts), depth, width), BF16),
            pltpu.VMEM((slots, width), BF16),
            pltpu.SemaphoreType.DMA((count,)),
            pltpu.SemaphoreType.DMA((len(experts),)),
            pltpu.SemaphoreType.DMA((slots // TILE,)),
        ],
        compiler_params=pltpu.CompilerParams(vmem_limit_bytes=VMEM),
        cost_estimate=pl.CostEstimate(
            flops=2 * slots * depth * width,
            bytes_accessed=2 * (depth * slots + depth * width + slots * width),
            transcendentals=0,
        ),
        name="down",
    )(*blocks, in_hbm(w_down))


def chunks_of(local_experts, capacity):
    size = local_experts * capacity // PARTS
    chunks = []
    for q in range(PARTS):
        runs, at = [], q * size
        while at < (q + 1) * size:
            j, c = at // capacity, at % capacity
            length = min((q + 1) * size - at, capacity - c)
            runs.append((j, c, length))
            at += length
        chunks.append(runs)
    return chunks


def layer(tokens, expert_ids, gate_probs, w_gate, w_up, w_down):
    tok_rows, width = tokens.shape
    top_count = expert_ids.shape[1]
    owners = lax.axis_size("expert")
    local_experts = w_gate.shape[0]
    expert_count = owners * local_experts
    capacity = 3 * tok_rows * top_count // (2 * expert_count)
    route = routing(expert_ids, gate_probs, expert_count, owners)
    size = local_experts * capacity // PARTS
    slots = owners * size
    total = jnp.zeros((tok_rows, width), F32)
    far_tokens = hop(tokens, lax.axis_size("etp") // CORES // 2, 0)

    for q, runs in enumerate(chunks_of(local_experts, capacity)):
        experts = tuple(j for j, _, _ in runs)
        group = runs[0][2]
        pick, mix = matrices(*route, runs)
        rows = jnp.concatenate([tokens, far_tokens], axis=1) if q else tokens
        outgoing = dot(pick.reshape(slots, tok_rows), rows, ((1,), (0,))).astype(BF16)
        arrived = lax.all_to_all(outgoing.reshape(owners, size, -1), "expert", 0, 0, tiled=True)
        hidden = gate_up(arrived.reshape(slots, -1), width, w_gate, w_up, experts, group)
        result = down(hidden, w_down, experts, group).reshape(owners, size, width)
        returned = lax.all_to_all(result, "expert", 0, 0, tiled=True).reshape(slots, width)
        parts = dot(mix.reshape(slots, 2 * tok_rows), returned, ((0,), (0,)))
        total = total + parts[:tok_rows] + parts[tok_rows:]
    return total.astype(BF16)


def solution(mesh):
    return jax.shard_map(
        layer,
        mesh=mesh,
        in_specs=(
            P("expert", "etp"),
            P("expert", None),
            P("expert", None),
            P("expert", "etp", None),
            P("expert", "etp", None),
            P("expert", None, "etp"),
        ),
        out_specs=P("expert", "etp"),
        check_vma=False,
    )
```

```python
import functools

import jax
import jax.numpy as jnp
from jax import lax
from jax.experimental import pallas as pl
from jax.experimental.pallas import tpu as pltpu
from jax.sharding import PartitionSpec as P


BF16 = jnp.bfloat16
F32 = jnp.float32
CORES = 2
TILE = 256
PARTS = 2
ALL = slice(None)
VMEM = 16 * 1024 * 1024


def dot(a, b, dims):
    return lax.dot_general(a, b, (dims, ((), ())), preferred_element_type=F32)


def dispatch_kernel(owners, run, ids_in, tokens, out, position, ids, rows, result, sems, osems):
    pulls = [pltpu.make_async_copy(ids_in, ids, sems.at[0]), pltpu.make_async_copy(tokens, rows, sems.at[1])]
    for cp in pulls:
        cp.start()
    expert_count, tok_rows = position.shape
    row = lax.broadcasted_iota(jnp.int32, position.shape, 0)
    expert = lax.rem(row, owners) * (expert_count // owners) + row // owners
    pulls[0].wait()
    member = expert == ids[0:1, :]
    for k in range(1, ids.shape[0]):
        member = member | (expert == ids[k : k + 1, :])
    member = jnp.where(member, 1.0, 0.0)
    square = (tok_rows, tok_rows)
    earlier = lax.broadcasted_iota(jnp.int32, square, 0) < lax.broadcasted_iota(jnp.int32, square, 1)
    before = dot(member.astype(BF16), jnp.where(earlier, 1.0, 0.0).astype(BF16), ((1,), (0,)))
    before = jnp.where(member > 0.0, before, -1.0)
    position[...] = before
    j, first, length = run
    slot = lax.broadcasted_iota(jnp.int32, (1, length, tok_rows), 1).astype(F32) + float(first)
    pulls[1].wait()
    puts = []
    part = owners // 4
    for i in range(4):
        at = pl.ds(i * part * length, part * length)
        mine = before[j * owners + i * part : j * owners + (i + 1) * part]
        chosen = jnp.where(mine[:, None, :] == slot, 1.0, 0.0).reshape(part * length, tok_rows)
        result[at, :] = dot(chosen.astype(BF16), rows[...], ((1,), (0,))).astype(BF16)
        puts.append(pltpu.make_async_copy(result.at[at], out.at[at], osems.at[i]))
        puts[-1].start()
    for cp in puts:
        cp.wait()


def dispatch(tokens, ids, owners, expert_count, run):
    tok_rows, width = tokens.shape
    slots = owners * run[2]
    return pl.pallas_call(
        functools.partial(dispatch_kernel, owners, run),
        out_shape=(
            jax.ShapeDtypeStruct((slots, width), BF16),
            jax.ShapeDtypeStruct((expert_count, tok_rows), F32),
        ),
        in_specs=[pl.BlockSpec(memory_space=pl.ANY)] * 2,
        out_specs=(pl.BlockSpec(memory_space=pl.ANY), pl.BlockSpec(memory_space=pltpu.VMEM)),
        scratch_shapes=[
            pltpu.VMEM(ids.shape, jnp.int32),
            pltpu.VMEM((tok_rows, width), BF16),
            pltpu.VMEM((slots, width), BF16),
            pltpu.SemaphoreType.DMA((2,)),
            pltpu.SemaphoreType.DMA((4,)),
        ],
        compiler_params=pltpu.CompilerParams(vmem_limit_bytes=VMEM),
        cost_estimate=pl.CostEstimate(
            flops=2 * slots * tok_rows * width, bytes_accessed=2 * slots * width, transcendentals=0
        ),
        name="dispatch",
    )(in_hbm(ids), in_hbm(tokens))


def gates(expert_ids, gate_probs, owners, expert_count):
    row = jnp.arange(expert_count, dtype=jnp.int32)
    experts = row % owners * (expert_count // owners) + row // owners
    hit = expert_ids.T[None] == experts[:, None, None]
    gate = jnp.sum(jnp.where(hit, gate_probs.T[None], 0.0), axis=1)
    high = lax.reduce_precision(gate, 8, 7)
    low = gate - high
    shape = (expert_count // owners, owners, 1, gate.shape[1])
    return high.astype(BF16).reshape(shape), low.astype(BF16).reshape(shape)


def matrices(position, high, low, runs):
    pick, mix = [], []
    for j, first, length in runs:
        slot = jnp.arange(first, first + length, dtype=jnp.int32).astype(F32)[None, :, None]
        chosen = position[j] == slot
        zero = jnp.zeros((), BF16)
        pick.append(chosen.astype(BF16))
        mix.append(jnp.concatenate([jnp.where(chosen, high[j], zero), jnp.where(chosen, low[j], zero)], axis=2))
    return jnp.concatenate(pick, axis=1), jnp.concatenate(mix, axis=1)


def hop(value, dx, flip):
    size = lax.axis_size("etp")
    chips = size // CORES
    pairs = []
    for x in range(chips):
        for c in range(CORES):
            pairs.append((x * CORES + c, ((x + dx) % chips) * CORES + (c ^ flip)))
    return lax.ppermute(value, "etp", pairs)


def in_hbm(value):
    return pltpu.with_memory_space_constraint(value, pltpu.HBM)


def swap(value):
    return hop(value, 0, 1)


def places(steps):
    chips = lax.axis_size("etp") // CORES
    me = lax.axis_index("etp")
    x, c = me // CORES, me % CORES
    back = [lax.rem(x + chips - dx, chips) * CORES for dx in steps]
    return [b + c for b in back] + [b + 1 - c for b in back]


def pick_expert(values, axis, group):
    if len(values) == 1:
        return values[0]
    slot = lax.broadcasted_iota(jnp.int32, values[0].shape, axis)
    turn = lax.rem(slot // group, len(values))
    out = values[0]
    for n in range(1, len(values)):
        out = jnp.where(turn == n, values[n], out)
    return out


def product_kernel(experts, group, steps, cores, wide, split, added, last, *refs):
    spots = places(steps)[cores]
    count = len(spots)
    pieces = refs[: count * split // wide]
    rest = refs[count * split // wide :]
    if added:
        wg, wu, prior, out, rows, weights, sems, wsems = rest
    else:
        wg, wu, out, rows, weights, sems, wsems = rest
    ff = wg.shape[1]
    height, width = pieces[0].shape[0], pieces[0].shape[1] // wide
    copies = []
    for b, place in enumerate(spots):
        lane = pl.multiple_of(place * width, width)
        for n, j in enumerate(experts):
            for half, w in enumerate((wg, wu)):
                copies.append(
                    pltpu.make_async_copy(
                        w.at[j, :, pl.ds(lane, width)],
                        weights.at[n, pl.ds(half * ff, ff), pl.ds(b * width, width)],
                        wsems.at[n, b, half],
                    )
                )

    tiles = height * split // TILE
    per = max(1, tiles // split) if split == 1 else 1
    step = height // per

    def pulls(i):
        out = []
        for b in range(count):
            for p in range(split):
                out.append(
                    pltpu.make_async_copy(
                        pieces[b // wide * split + p].at[
                            pl.ds(pl.multiple_of(i * step, step), step), pl.ds(b % wide * width, width)
                        ],
                        rows.at[pl.ds(pl.multiple_of(p * height + i * step, step), step), pl.ds(b * width, width)],
                        sems.at[i, b, p],
                    )
                )
        return out

    for cp in copies:
        cp.start()
    for i in range(per):
        for cp in pulls(i):
            cp.start()
    for cp in copies:
        cp.wait()
    if per == 1:
        for cp in pulls(0):
            cp.wait()

    @pl.loop(0, tiles)
    def _(i):
        if per > 1:
            for cp in pulls(i):
                cp.wait()
        at = pl.ds(pl.multiple_of(i * TILE, TILE), TILE)
        both = [dot(weights[n], rows[at, :], ((1,), (1,))) for n in range(len(experts))]
        both = pick_expert(both, 1, group)
        if added:
            both = both + prior[:, at]
        if last:
            gate, upper = both[:ff], both[ff:]
            out[:, at] = (gate / (1.0 + jnp.exp(-gate)) * upper).astype(BF16)
        else:
            out[:, at] = both


def product(pieces, wide, steps, split, w_gate, w_up, experts, group, prior=None, cores=ALL, last=False):
    count = len(pieces) * wide // split
    height, width = pieces[0].shape[0], pieces[0].shape[1] // wide
    slots = height * split
    ff = w_gate.shape[1]
    added = prior is not None
    hbm = pl.BlockSpec(memory_space=pl.ANY)
    vmem = pl.BlockSpec(memory_space=pltpu.VMEM)
    shape = jax.ShapeDtypeStruct((ff, slots), BF16) if last else jax.ShapeDtypeStruct((2 * ff, slots), F32)
    return pl.pallas_call(
        functools.partial(product_kernel, experts, group, steps, cores, wide, split, added, last),
        out_shape=shape,
        in_specs=[hbm] * (len(pieces) + 2) + ([vmem] if added else []),
        out_specs=vmem,
        scratch_shapes=[
            pltpu.VMEM((slots, count * width), BF16),
            pltpu.VMEM((len(experts), 2 * ff, count * width), BF16),
            pltpu.SemaphoreType.DMA((slots // TILE, count, split)),
            pltpu.SemaphoreType.DMA((len(experts), count, 2)),
        ],
        compiler_params=pltpu.CompilerParams(vmem_limit_bytes=VMEM),
        cost_estimate=pl.CostEstimate(
            flops=4 * slots * count * width * ff,
            bytes_accessed=2 * count * width * (slots + 2 * ff) + 4 * 2 * ff * slots,
            transcendentals=slots * ff if last else 0,
        ),
        name="gate_up_last" if last else "gate_up_first",
    )(*pieces, in_hbm(w_gate), in_hbm(w_up), *([prior] if added else []))


def gate_up(arrived, width, w_gate, w_up, experts, group):
    wide = arrived.shape[1] // width
    own = arrived[:, :width]
    half = own.shape[0] // 2
    ahead, behind = hop(own, 1, 0), hop(own, -1, 0)
    partner = swap(arrived)
    swapped = [swap(ahead), swap(behind)]
    if wide == 1:
        far = [hop(ahead[:half], 1, 0), hop(behind[half:], -1, 0)]
        late = far + [swap(b) for b in far]
        early, early_steps, late_steps, split = [own, ahead, behind, partner, *swapped], (0, 1, -1), (2,), 2
    else:
        early, late = [arrived, partner], swapped
        early_steps, late_steps, split = (0, 2), (1, -1), 1
    acc = product(early, wide, early_steps, 1, w_gate, w_up, experts, group)
    cores = ALL
    if wide > 1:
        acc = product([ahead, behind], 1, late_steps, 1, w_gate, w_up, experts, group, acc, slice(0, 2))
        cores = slice(2, 4)
    return product(late, 1, late_steps, split, w_gate, w_up, experts, group, acc, cores, True)


def down_kernel(experts, group, count, *refs):
    blocks = refs[:count]
    wd, out, hidden, weights, result, sems, wsems, osems = refs[count:]
    ff, slots = blocks[0].shape
    copies = [pltpu.make_async_copy(wd.at[j], weights.at[n], wsems.at[n]) for n, j in enumerate(experts)]
    for b, place in enumerate(places(range(count // CORES))):
        at = pl.multiple_of(place * ff, ff)
        copies.append(pltpu.make_async_copy(blocks[b], hidden.at[pl.ds(at, ff)], sems.at[b]))
    for cp in copies:
        cp.start()
    for cp in copies:
        cp.wait()

    outs = []
    for i in range(slots // TILE):
        at = pl.ds(i * TILE, TILE)
        part = [dot(hidden[:, at], weights[n], ((0,), (0,))) for n in range(len(experts))]
        result[at, :] = pick_expert(part, 0, group).astype(BF16)
        outs.append(pltpu.make_async_copy(result.at[at], out.at[at], osems.at[i]))
        outs[-1].start()
    for cp in outs:
        cp.wait()


def down(hidden, w_down, experts, group):
    one, back = hop(hidden, 1, 0), hop(hidden, -1, 0)
    blocks = [hidden, one, hop(hidden, 2, 0), back]
    partner = swap(hidden)
    blocks = blocks + [partner] + [swap(b) for b in blocks[1:]]
    count = len(blocks)
    _, slots = hidden.shape
    depth, width = w_down.shape[1:]
    hbm = pl.BlockSpec(memory_space=pl.ANY)
    return pl.pallas_call(
        functools.partial(down_kernel, experts, group, count),
        out_shape=jax.ShapeDtypeStruct((slots, width), BF16),
        in_specs=[hbm] * (count + 1),
        out_specs=hbm,
        scratch_shapes=[
            pltpu.VMEM((depth, slots), BF16),
            pltpu.VMEM((len(experts), depth, width), BF16),
            pltpu.VMEM((slots, width), BF16),
            pltpu.SemaphoreType.DMA((count,)),
            pltpu.SemaphoreType.DMA((len(experts),)),
            pltpu.SemaphoreType.DMA((slots // TILE,)),
        ],
        compiler_params=pltpu.CompilerParams(vmem_limit_bytes=VMEM),
        cost_estimate=pl.CostEstimate(
            flops=2 * slots * depth * width,
            bytes_accessed=2 * (depth * slots + depth * width + slots * width),
            transcendentals=0,
        ),
        name="down",
    )(*blocks, in_hbm(w_down))


def chunks_of(local_experts, capacity):
    size = local_experts * capacity // PARTS
    chunks = []
    for q in range(PARTS):
        runs, at = [], q * size
        while at < (q + 1) * size:
            j, c = at // capacity, at % capacity
            length = min((q + 1) * size - at, capacity - c)
            runs.append((j, c, length))
            at += length
        chunks.append(runs)
    return chunks


def layer(tokens, expert_ids, gate_probs, w_gate, w_up, w_down):
    tok_rows, width = tokens.shape
    top_count = expert_ids.shape[1]
    owners = lax.axis_size("expert")
    local_experts = w_gate.shape[0]
    expert_count = owners * local_experts
    capacity = 3 * tok_rows * top_count // (2 * expert_count)
    chunks = chunks_of(local_experts, capacity)
    outgoing, position = dispatch(tokens, expert_ids.T, owners, expert_count, chunks[0][0])
    position = position.reshape(local_experts, owners, 1, tok_rows)
    high, low = gates(expert_ids, gate_probs, owners, expert_count)
    size = local_experts * capacity // PARTS
    slots = owners * size
    total = jnp.zeros((tok_rows, width), F32)
    far_tokens = hop(tokens, lax.axis_size("etp") // CORES // 2, 0)

    for q, runs in enumerate(chunks):
        experts = tuple(j for j, _, _ in runs)
        group = runs[0][2]
        pick, mix = matrices(position, high, low, runs)
        if q:
            rows = jnp.concatenate([tokens, far_tokens], axis=1)
            outgoing = dot(pick.reshape(slots, tok_rows), rows, ((1,), (0,))).astype(BF16)
        arrived = lax.all_to_all(outgoing.reshape(owners, size, -1), "expert", 0, 0, tiled=True)
        hidden = gate_up(arrived.reshape(slots, -1), width, w_gate, w_up, experts, group)
        result = down(hidden, w_down, experts, group).reshape(owners, size, width)
        returned = lax.all_to_all(result, "expert", 0, 0, tiled=True).reshape(slots, width)
        parts = dot(mix.reshape(slots, 2 * tok_rows), returned, ((0,), (0,)))
        total = total + parts[:tok_rows] + parts[tok_rows:]
    return total.astype(BF16)


def solution(mesh):
    return jax.shard_map(
        layer,
        mesh=mesh,
        in_specs=(
            P("expert", "etp"),
            P("expert", None),
            P("expert", None),
            P("expert", "etp", None),
            P("expert", "etp", None),
            P("expert", None, "etp"),
        ),
        out_specs=P("expert", "etp"),
        check_vma=False,
    )
```

```python
import functools

import jax
import jax.numpy as jnp
from jax import lax
from jax.experimental import pallas as pl
from jax.experimental.pallas import tpu as pltpu
from jax.sharding import PartitionSpec as P


BF16 = jnp.bfloat16
F32 = jnp.float32
CORES = 2
TILE = 256
PARTS = 2
ALL = slice(None)
VMEM = 16 * 1024 * 1024


def dot(a, b, dims):
    return lax.dot_general(a, b, (dims, ((), ())), preferred_element_type=F32)


def dispatch_kernel(owners, run, ids_in, tokens, out, position, ids, rows, result, sems, osems):
    pulls = [pltpu.make_async_copy(ids_in, ids, sems.at[0]), pltpu.make_async_copy(tokens, rows, sems.at[1])]
    for cp in pulls:
        cp.start()
    expert_count, tok_rows = position.shape
    row = lax.broadcasted_iota(jnp.int32, position.shape, 0)
    expert = lax.rem(row, owners) * (expert_count // owners) + row // owners
    pulls[0].wait()
    member = expert == ids[0:1, :]
    for k in range(1, ids.shape[0]):
        member = member | (expert == ids[k : k + 1, :])
    member = jnp.where(member, 1.0, 0.0)
    square = (tok_rows, tok_rows)
    earlier = lax.broadcasted_iota(jnp.int32, square, 0) < lax.broadcasted_iota(jnp.int32, square, 1)
    before = dot(member.astype(BF16), jnp.where(earlier, 1.0, 0.0).astype(BF16), ((1,), (0,)))
    before = jnp.where(member > 0.0, before, -1.0)
    position[...] = before
    j, first, length = run
    slot = lax.broadcasted_iota(jnp.int32, (1, length, tok_rows), 1).astype(F32) + float(first)
    pulls[1].wait()
    puts = []
    part = owners // 4
    for i in range(4):
        at = pl.ds(i * part * length, part * length)
        mine = before[j * owners + i * part : j * owners + (i + 1) * part]
        chosen = jnp.where(mine[:, None, :] == slot, 1.0, 0.0).reshape(part * length, tok_rows)
        result[at, :] = dot(chosen.astype(BF16), rows[...], ((1,), (0,))).astype(BF16)
        puts.append(pltpu.make_async_copy(result.at[at], out.at[at], osems.at[i]))
        puts[-1].start()
    for cp in puts:
        cp.wait()


def dispatch(tokens, ids, owners, expert_count, run):
    tok_rows, width = tokens.shape
    slots = owners * run[2]
    return pl.pallas_call(
        functools.partial(dispatch_kernel, owners, run),
        out_shape=(
            jax.ShapeDtypeStruct((slots, width), BF16),
            jax.ShapeDtypeStruct((expert_count, tok_rows), F32),
        ),
        in_specs=[pl.BlockSpec(memory_space=pl.ANY)] * 2,
        out_specs=(pl.BlockSpec(memory_space=pl.ANY), pl.BlockSpec(memory_space=pltpu.VMEM)),
        scratch_shapes=[
            pltpu.VMEM(ids.shape, jnp.int32),
            pltpu.VMEM((tok_rows, width), BF16),
            pltpu.VMEM((slots, width), BF16),
            pltpu.SemaphoreType.DMA((2,)),
            pltpu.SemaphoreType.DMA((4,)),
        ],
        compiler_params=pltpu.CompilerParams(vmem_limit_bytes=VMEM),
        cost_estimate=pl.CostEstimate(
            flops=2 * slots * tok_rows * width, bytes_accessed=2 * slots * width, transcendentals=0
        ),
        name="dispatch",
    )(in_hbm(ids), in_hbm(tokens))


def gates(expert_ids, gate_probs, owners, expert_count):
    row = jnp.arange(expert_count, dtype=jnp.int32)
    experts = row % owners * (expert_count // owners) + row // owners
    hit = expert_ids.T[None] == experts[:, None, None]
    gate = jnp.sum(jnp.where(hit, gate_probs.T[None], 0.0), axis=1)
    high = lax.reduce_precision(gate, 8, 7)
    low = gate - high
    shape = (expert_count // owners, owners, 1, gate.shape[1])
    return high.astype(BF16).reshape(shape), low.astype(BF16).reshape(shape)


def matrices(position, high, low, runs):
    pick, mix = [], []
    for j, first, length in runs:
        slot = jnp.arange(first, first + length, dtype=jnp.int32).astype(F32)[None, :, None]
        chosen = position[j] == slot
        zero = jnp.zeros((), BF16)
        pick.append(chosen.astype(BF16))
        mix.append(jnp.concatenate([jnp.where(chosen, high[j], zero), jnp.where(chosen, low[j], zero)], axis=2))
    return jnp.concatenate(pick, axis=1), jnp.concatenate(mix, axis=1)


def hop(value, dx, flip):
    size = lax.axis_size("etp")
    chips = size // CORES
    pairs = []
    for x in range(chips):
        for c in range(CORES):
            pairs.append((x * CORES + c, ((x + dx) % chips) * CORES + (c ^ flip)))
    return lax.ppermute(value, "etp", pairs)


def in_hbm(value):
    return pltpu.with_memory_space_constraint(value, pltpu.HBM)


def swap(value):
    return hop(value, 0, 1)


def places(steps):
    chips = lax.axis_size("etp") // CORES
    me = lax.axis_index("etp")
    x, c = me // CORES, me % CORES
    back = [lax.rem(x + chips - dx, chips) * CORES for dx in steps]
    return [b + c for b in back] + [b + 1 - c for b in back]


def pick_expert(values, axis, group):
    if len(values) == 1:
        return values[0]
    slot = lax.broadcasted_iota(jnp.int32, values[0].shape, axis)
    turn = lax.rem(slot // group, len(values))
    out = values[0]
    for n in range(1, len(values)):
        out = jnp.where(turn == n, values[n], out)
    return out


def product_kernel(experts, group, steps, cores, wide, split, added, last, *refs):
    spots = places(steps)[cores]
    count = len(spots)
    pieces = refs[: count * split // wide]
    rest = refs[count * split // wide :]
    if added:
        wg, wu, prior, out, rows, weights, sems, wsems = rest
    else:
        wg, wu, out, rows, weights, sems, wsems = rest
    ff = wg.shape[1]
    height, width = pieces[0].shape[0], pieces[0].shape[1] // wide
    copies = []
    for b, place in enumerate(spots):
        lane = pl.multiple_of(place * width, width)
        for n, j in enumerate(experts):
            for half, w in enumerate((wg, wu)):
                copies.append(
                    pltpu.make_async_copy(
                        w.at[j, :, pl.ds(lane, width)],
                        weights.at[n, pl.ds(half * ff, ff), pl.ds(b * width, width)],
                        wsems.at[n, b, half],
                    )
                )

    tiles = height * split // TILE
    per = max(1, tiles // split) if split == 1 else 1
    step = height // per

    def pulls(i):
        out = []
        for b in range(count):
            for p in range(split):
                out.append(
                    pltpu.make_async_copy(
                        pieces[b // wide * split + p].at[
                            pl.ds(pl.multiple_of(i * step, step), step), pl.ds(b % wide * width, width)
                        ],
                        rows.at[pl.ds(pl.multiple_of(p * height + i * step, step), step), pl.ds(b * width, width)],
                        sems.at[i, b, p],
                    )
                )
        return out

    for cp in copies:
        cp.start()
    for i in range(per):
        for cp in pulls(i):
            cp.start()
    for cp in copies:
        cp.wait()
    if per == 1:
        for cp in pulls(0):
            cp.wait()

    @pl.loop(0, tiles)
    def _(i):
        if per > 1:
            for cp in pulls(i):
                cp.wait()
        at = pl.ds(pl.multiple_of(i * TILE, TILE), TILE)
        both = [dot(weights[n], rows[at, :], ((1,), (1,))) for n in range(len(experts))]
        both = pick_expert(both, 1, group)
        if added:
            both = both + prior[:, at]
        if last:
            gate, upper = both[:ff], both[ff:]
            out[:, at] = (gate / (1.0 + jnp.exp(-gate)) * upper).astype(BF16)
        else:
            out[:, at] = both


def product(pieces, wide, steps, split, w_gate, w_up, experts, group, prior=None, cores=ALL, last=False):
    count = len(pieces) * wide // split
    height, width = pieces[0].shape[0], pieces[0].shape[1] // wide
    slots = height * split
    ff = w_gate.shape[1]
    added = prior is not None
    hbm = pl.BlockSpec(memory_space=pl.ANY)
    vmem = pl.BlockSpec(memory_space=pltpu.VMEM)
    shape = jax.ShapeDtypeStruct((ff, slots), BF16) if last else jax.ShapeDtypeStruct((2 * ff, slots), F32)
    return pl.pallas_call(
        functools.partial(product_kernel, experts, group, steps, cores, wide, split, added, last),
        out_shape=shape,
        in_specs=[hbm] * (len(pieces) + 2) + ([vmem] if added else []),
        out_specs=vmem,
        scratch_shapes=[
            pltpu.VMEM((slots, count * width), BF16),
            pltpu.VMEM((len(experts), 2 * ff, count * width), BF16),
            pltpu.SemaphoreType.DMA((slots // TILE, count, split)),
            pltpu.SemaphoreType.DMA((len(experts), count, 2)),
        ],
        compiler_params=pltpu.CompilerParams(vmem_limit_bytes=VMEM),
        cost_estimate=pl.CostEstimate(
            flops=4 * slots * count * width * ff,
            bytes_accessed=2 * count * width * (slots + 2 * ff) + 4 * 2 * ff * slots,
            transcendentals=slots * ff if last else 0,
        ),
        name="gate_up_last" if last else "gate_up_first",
    )(*pieces, in_hbm(w_gate), in_hbm(w_up), *([prior] if added else []))


def gate_up(arrived, width, w_gate, w_up, experts, group):
    wide = arrived.shape[1] // width
    own = arrived[:, :width]
    half = own.shape[0] // 2
    ahead, behind = hop(own, 1, 0), hop(own, -1, 0)
    partner = swap(arrived)
    swapped = [swap(ahead), swap(behind)]
    if wide == 1:
        far = [hop(ahead[:half], 1, 0), hop(behind[half:], -1, 0)]
        late = [swap(b) for b in far]
        early, middle = [own, ahead, behind, partner, *swapped], far
        early_steps, late_steps, split = (0, 1, -1), (2,), 2
    else:
        early, middle, late = [arrived, partner], [ahead, behind], swapped
        early_steps, late_steps, split = (0, 2), (1, -1), 1
    near_core, far_core = slice(0, len(late_steps)), slice(len(late_steps), None)
    acc = product(early, wide, early_steps, 1, w_gate, w_up, experts, group)
    acc = product(middle, 1, late_steps, split, w_gate, w_up, experts, group, acc, near_core)
    return product(late, 1, late_steps, split, w_gate, w_up, experts, group, acc, far_core, True)


def down_kernel(experts, group, cores, added, *refs):
    spots = places(range(lax.axis_size("etp") // CORES))[cores]
    count = len(spots)
    blocks, wd = refs[:count], refs[count]
    if added:
        prior, out, hidden, weights, sems, wsems, result, osems = refs[count + 1 :]
    else:
        out, hidden, weights, sems, wsems = refs[count + 1 :]
    ff, slots = blocks[0].shape
    copies = []
    for b, spot in enumerate(spots):
        here = pl.ds(b * ff, ff)
        for n, j in enumerate(experts):
            there = pl.ds(pl.multiple_of(spot * ff, ff), ff)
            copies.append(pltpu.make_async_copy(wd.at[j, there], weights.at[n, here], wsems.at[n, b]))
        copies.append(pltpu.make_async_copy(blocks[b], hidden.at[here], sems.at[b]))
    for cp in copies:
        cp.start()
    for cp in copies:
        cp.wait()
    outs = []
    for i in range(slots // TILE):
        at = pl.ds(i * TILE, TILE)
        part = pick_expert([dot(hidden[:, at], weights[n], ((0,), (0,))) for n in range(len(experts))], 0, group)
        if added:
            result[at, :] = (part + prior[at, :]).astype(BF16)
            outs.append(pltpu.make_async_copy(result.at[at], out.at[at], osems.at[i]))
            outs[-1].start()
        else:
            out[at, :] = part
    for cp in outs:
        cp.wait()


def down_part(blocks, w_down, experts, group, cores, prior=None):
    count = len(blocks)
    ff, slots = blocks[0].shape
    width = w_down.shape[2]
    hbm = pl.BlockSpec(memory_space=pl.ANY)
    vmem = pl.BlockSpec(memory_space=pltpu.VMEM)
    added = prior is not None
    scratch = [
        pltpu.VMEM((count * ff, slots), BF16),
        pltpu.VMEM((len(experts), count * ff, width), BF16),
        pltpu.SemaphoreType.DMA((count,)),
        pltpu.SemaphoreType.DMA((len(experts), count)),
    ]
    if added:
        scratch += [pltpu.VMEM((slots, width), BF16), pltpu.SemaphoreType.DMA((slots // TILE,))]
    return pl.pallas_call(
        functools.partial(down_kernel, experts, group, cores, added),
        out_shape=jax.ShapeDtypeStruct((slots, width), BF16 if added else F32),
        in_specs=[hbm] * (count + 1) + ([vmem] if added else []),
        out_specs=hbm if added else vmem,
        scratch_shapes=scratch,
        compiler_params=pltpu.CompilerParams(vmem_limit_bytes=VMEM),
        cost_estimate=pl.CostEstimate(
            flops=2 * slots * count * ff * width,
            bytes_accessed=2 * (count * ff * (slots + width) + slots * width),
            transcendentals=0,
        ),
        name="down_last" if added else "down_first",
    )(*blocks, in_hbm(w_down), *([prior] if added else []))


def down(hidden, w_down, experts, group):
    two = hop(hidden, 2, 0)
    same = [hidden, hop(hidden, 1, 0), two, hop(hidden, -1, 0)]
    partner = swap(hidden)
    other = [partner] + [swap(b) for b in same[1:]]
    acc = down_part(same, w_down, experts, group, slice(0, len(same)))
    return down_part(other, w_down, experts, group, slice(len(same), None), acc)


def chunks_of(local_experts, capacity):
    size = local_experts * capacity // PARTS
    chunks = []
    for q in range(PARTS):
        runs, at = [], q * size
        while at < (q + 1) * size:
            j, c = at // capacity, at % capacity
            length = min((q + 1) * size - at, capacity - c)
            runs.append((j, c, length))
            at += length
        chunks.append(runs)
    return chunks


def layer(tokens, expert_ids, gate_probs, w_gate, w_up, w_down):
    tok_rows, width = tokens.shape
    top_count = expert_ids.shape[1]
    owners = lax.axis_size("expert")
    local_experts = w_gate.shape[0]
    expert_count = owners * local_experts
    capacity = 3 * tok_rows * top_count // (2 * expert_count)
    chunks = chunks_of(local_experts, capacity)
    outgoing, position = dispatch(tokens, expert_ids.T, owners, expert_count, chunks[0][0])
    position = position.reshape(local_experts, owners, 1, tok_rows)
    high, low = gates(expert_ids, gate_probs, owners, expert_count)
    size = local_experts * capacity // PARTS
    slots = owners * size
    total = jnp.zeros((tok_rows, width), F32)
    far_tokens = hop(tokens, lax.axis_size("etp") // CORES // 2, 0)

    for q, runs in enumerate(chunks):
        experts = tuple(j for j, _, _ in runs)
        group = runs[0][2]
        pick, mix = matrices(position, high, low, runs)
        if q:
            rows = jnp.concatenate([tokens, far_tokens], axis=1)
            outgoing = dot(pick.reshape(slots, tok_rows), rows, ((1,), (0,))).astype(BF16)
        arrived = lax.all_to_all(outgoing.reshape(owners, size, -1), "expert", 0, 0, tiled=True)
        hidden = gate_up(arrived.reshape(slots, -1), width, w_gate, w_up, experts, group)
        result = down(hidden, w_down, experts, group).reshape(owners, size, width)
        returned = lax.all_to_all(result, "expert", 0, 0, tiled=True).reshape(slots, width)
        parts = dot(mix.reshape(slots, 2 * tok_rows), returned, ((0,), (0,)))
        total = total + parts[:tok_rows] + parts[tok_rows:]
        if q + 1 < len(chunks):
            total = lax.optimization_barrier(total)
    return total.astype(BF16)


def solution(mesh):
    return jax.shard_map(
        layer,
        mesh=mesh,
        in_specs=(
            P("expert", "etp"),
            P("expert", None),
            P("expert", None),
            P("expert", "etp", None),
            P("expert", "etp", None),
            P("expert", None, "etp"),
        ),
        out_specs=P("expert", "etp"),
        check_vma=False,
    )
```
